32 devices in a mesh: grp: 2 (over y), garm: 4 (over z), body: 2 (over x), frame: 2 (over core).
Axes of the slice: x: 2, y: 2, z: 4, core: 2. Of those that a mesh axis runs over, the one named last changes fastest.
Arguments:
- garment: float32 [4, 3, 32768], P(('grp', 'frame'), None, ('garm', 'body')), parts along dimension 0, may hold values from -6 to 6
- cotangent: float32 [4, 32768], P(('grp', 'frame'), ('garm', 'body')), parts along dimension 0, may hold values from -6 to 6
- body_points: float32 [4, 3, 16384], P(('grp', 'frame'), None, ('garm', 'body')), parts along dimension 0, may hold values from -6 to 6
- stiffness: float32 [32768], P(('grp', 'garm', 'body')), parts along dimension 0, may hold values from 0.2 to 2
- pair_garment: int32 [4, 8, 8, 4], P(('grp', 'frame'), ('garm', 'body')), parts along dimension 0, may hold values from 0 to 31
- pair_body: int32 [4, 8, 8, 4], P(('grp', 'frame'), ('garm', 'body')), parts along dimension 0, may hold values from 0 to 15
- pair_count: int32 [4, 8, 8], P(('grp', 'frame'), ('garm', 'body')), parts along dimension 0, may hold values from 0 to 4, as said below
Outputs:
- garment_grad: float32 [4, 3, 32768], P(('grp', 'frame'), None, ('garm', 'body')), parts along dimension 0
- body_grad: float32 [4, 3, 16384], P(('grp', 'frame'), None, ('garm', 'body')), parts along dimension 0
- stiffness_grad: float32 [32768], P(('grp', 'garm', 'body')), parts along dimension 0
The draws below stay inside these ranges and needn't reach their ends.
There are 2 independent parts, one for each index of `grp`. The reference program is written for one: setup_inputs(seed, part) draws one part's arguments, and reference() takes and returns one part's arrays. A program takes and returns all parts, laid end to end along the dimension named above; each array names one. Nothing has to cross between parts.
Inputs may be any that keep to these rules, and one draw needn't show every extreme that they name: pair_count gives the live slots; in every frame one receiving owner gets 4 live slots from every sending owner. `pair_garment`: slots at or past the count are unused and hold arbitrary block numbers. `pair_body`: slots at or past the count are unused and hold arbitrary block numbers.
All inputs are finite; a program needn't handle non-finite values.
Results may differ from the reference program's by a relative error of at most 0.00016.
Values sent between devices are 32-bit elements; how exact they have to be, the bound alone decides.
A program may use at most 64 MiB of HBM per device.

```python
import math
import jax
import jax.numpy as jnp
from jax import lax

BLOCK = 128
CAP = 4
GB_DEV = 32
BB_DEV = 16
OWNERS = 8
FRAMES = 2
VERTS = 32768
POINTS = 16384


def draw_pair_count(key, part):
    key_level = jax.random.fold_in(key, 11)
    key_raw = jax.random.fold_in(key, 12)
    key_hot = jax.random.fold_in(key, 13)
    level = jax.random.randint(key_level, (FRAMES, 1, OWNERS), 1, CAP + 1)
    raw_draw = jax.random.randint(key_raw, (FRAMES, OWNERS, OWNERS), 0, 2 * CAP + 1)
    counts = jnp.minimum(raw_draw * level // CAP, CAP)
    hottest = jax.random.randint(key_hot, (FRAMES, 1, 1), 0, OWNERS)
    owner_ids = jnp.arange(OWNERS, dtype=jnp.int32)[None, None, :]
    counts = jnp.where(owner_ids == hottest, CAP, counts)
    return counts.astype(jnp.int32)


def set_ends(values, rng, smallest, top_value):
    dims = values.shape
    spot = [jax.random.randint(jax.random.fold_in(rng, axis), (), 0, dims[axis]) for axis in range(len(dims))]
    values = values.at[tuple(spot)].set(smallest)
    longest = dims.index(max(dims))
    spot[longest] = (spot[longest] + 1) % dims[longest]
    return values.at[tuple(spot)].set(top_value)


def block_levels(own_key, extent, split, smallest, top_value):
    def one(position, blocks):
        draws = jax.random.uniform(jax.random.fold_in(jax.random.fold_in(own_key, 6), position), (blocks,), jnp.float32, smallest / len(split), top_value / len(split))
        return jnp.repeat(jnp.exp(draws), extent[position] // blocks).reshape((-1,) + (1,) * (len(extent) - position - 1))

    level = one(*split[0])
    for cut in split[1:]:
        level = level * one(*cut)
    return level


def centred(stream_key, shape, spread, reach, split=(), kind=jnp.bfloat16):
    result = jax.random.normal(stream_key, shape, jnp.float32) * spread
    if len(split) > 0:
        result = block_levels(stream_key, shape, split, -0.22, 0.18) * result
    return jnp.clip(result, min=-reach, max=reach).astype(kind)


def setup_inputs(seed: int = 0, part: int = 0) -> dict:
    streams_of = jax.random.split(jax.random.key(seed), 8)
    part_splits = jax.random.split(jax.random.fold_in(streams_of[7], part), 8)
    return {
        "garment": centred(part_splits[0], (FRAMES, 3, VERTS), 1.0, 6.0, ((0, 2), (2, 8)), jnp.float32),
        "cotangent": centred(part_splits[1], (FRAMES, VERTS), 1.0, 6.0, ((0, 2), (1, 8)), jnp.float32),
        "body_points": centred(part_splits[2], (FRAMES, 3, POINTS), 1.0, 6.0, ((0, 2), (2, 8)), jnp.float32),
        "stiffness": jnp.clip(jnp.exp(math.log(2.0) - 2.3025851 * jax.random.uniform(part_splits[3], (POINTS,), jnp.float32) ** block_levels(part_splits[3], (POINTS,), ((0, 8),), -0.2, 0.2)), 0.2, 2.0),
        "pair_garment": set_ends(jax.random.randint(part_splits[4], (FRAMES, OWNERS, OWNERS, CAP), 0, GB_DEV), jax.random.fold_in(part_splits[4], 1), 0, GB_DEV - 1).astype(jnp.int32),
        "pair_body": set_ends(jax.random.randint(part_splits[5], (FRAMES, OWNERS, OWNERS, CAP), 0, BB_DEV), jax.random.fold_in(part_splits[5], 1), 0, BB_DEV - 1).astype(jnp.int32),
        "pair_count": draw_pair_count(jax.random.fold_in(jax.random.fold_in(streams_of[7], part), 71), part),
    }


amplitude = 0.05
width_sq = 4.0


def pair_terms(garm_pos, cot_vals, body_pos, stiff_vals):
    distance = jnp.zeros((garm_pos.shape[0], garm_pos.shape[2], body_pos.shape[2]), jnp.float32)
    for coord in range(3):
        delta = garm_pos[:, coord, :, None] - body_pos[:, coord, None, :]
        distance = distance + delta * delta
    kernel = jnp.exp(-distance / width_sq)
    coupled = amplitude * cot_vals[:, :, None] * stiff_vals[:, None, :] * kernel
    row_sums = jnp.sum(coupled, axis=2)
    col_sums = jnp.sum(coupled, axis=1)
    pulled_body = jnp.einsum('nij,naj->nai', coupled, body_pos, precision=lax.Precision.HIGHEST)
    pulled_garm = jnp.einsum('nij,nai->naj', coupled, garm_pos, precision=lax.Precision.HIGHEST)
    factor = -2.0 / width_sq
    garm_grad = factor * (garm_pos * row_sums[:, None, :] - pulled_body)
    body_part = factor * (body_pos * col_sums[:, None, :] - pulled_garm)
    stiff_part = amplitude * jnp.einsum('ni,nij->nj', cot_vals, kernel, precision=lax.Precision.HIGHEST)
    return garm_grad, body_part, stiff_part


def reference(garment, cotangent, body_points, stiffness, pair_garment, pair_body, pair_count):
    owners = OWNERS
    garm_blocks = owners * GB_DEV
    body_blocks = owners * BB_DEV
    slot_ids = jnp.arange(CAP, dtype=jnp.int32)
    is_live = (slot_ids[None, None, None, :] < pair_count[:, :, :, None]).astype(jnp.float32)
    source = jnp.arange(owners, dtype=jnp.int32)[None, :, None, None]
    target = jnp.arange(owners, dtype=jnp.int32)[None, None, :, None]
    garm_index = (source * GB_DEV + pair_garment).astype(jnp.int32).reshape(FRAMES, owners, owners * CAP)
    body_index = (target * BB_DEV + pair_body).astype(jnp.int32).reshape(FRAMES, owners, owners * CAP)
    weight = is_live.reshape(FRAMES, owners, owners * CAP)
    garm_table = garment.reshape(FRAMES, 3, garm_blocks, BLOCK).transpose(0, 2, 1, 3)
    cot_table = cotangent.reshape(FRAMES, garm_blocks, BLOCK)
    body_table = body_points.reshape(FRAMES, 3, body_blocks, BLOCK).transpose(0, 2, 1, 3)
    stiff_table = stiffness.reshape(body_blocks, BLOCK)
    garm_out = []
    body_out = []
    stiff_total = jnp.zeros((body_blocks, BLOCK), jnp.float32)
    for frame_idx in range(FRAMES):
        garm_here = garm_table[frame_idx]
        cot_here = cot_table[frame_idx]
        body_here = body_table[frame_idx]

        def advance(running, inputs):
            garm_acc, body_acc, stiff_acc = running
            garm_ids, body_ids, live_wt = inputs
            garm_grad, body_part, stiff_part = pair_terms(garm_here[garm_ids], cot_here[garm_ids] * live_wt[:, None], body_here[body_ids], stiff_table[body_ids])
            return (garm_acc.at[garm_ids].add(garm_grad), body_acc.at[body_ids].add(body_part), stiff_acc.at[body_ids].add(stiff_part)), None

        start = (jnp.zeros((garm_blocks, 3, BLOCK), jnp.float32), jnp.zeros((body_blocks, 3, BLOCK), jnp.float32), jnp.zeros((body_blocks, BLOCK), jnp.float32))
        (garm_acc, body_acc, stiff_acc), _ = lax.scan(advance, start, (garm_index[frame_idx], body_index[frame_idx], weight[frame_idx]))
        garm_out.append(garm_acc.transpose(1, 0, 2).reshape(3, garm_blocks * BLOCK))
        body_out.append(body_acc.transpose(1, 0, 2).reshape(3, body_blocks * BLOCK))
        stiff_total = stiff_total + stiff_acc
    return jnp.stack(garm_out), jnp.stack(body_out), stiff_total.reshape(body_blocks * BLOCK)
```

```python
import functools
import math

import jax
import jax.numpy as jnp
from jax import lax
from jax.experimental import pallas as pl
from jax.experimental.pallas import tpu as pltpu
from jax.sharding import PartitionSpec as P

BLOCK = 128
amplitude = 0.05
width_sq = 4.0
SCALE = math.sqrt(math.log2(math.e) / width_sq)
GRAD = -2.0 / width_sq * amplitude / SCALE
GROUP = 8
MESH = pl.DeviceIdType.MESH
BF = jnp.bfloat16
F32 = jnp.float32


def split3(v):
    hi = v.astype(BF)
    rest = v - hi.astype(F32)
    mid = rest.astype(BF)
    return hi, mid, (rest - mid.astype(F32)).astype(BF)


def dot(a, b):
    return jnp.dot(a, b, preferred_element_type=F32)


def dot_t(a, b):
    return lax.dot_general(a, b, (((1,), (1,)), ((), ())), preferred_element_type=F32)


def each(count, body):
    if count <= 8:
        for k in range(count):
            body(k)
    else:
        lax.fori_loop(0, count, lambda k, c: (body(k), c)[1], 0)


def kernel(owners, inner, cap, gb, bb, *refs):
    hbm, refs = refs[:7], refs[7:]
    (out_g, out_b, out_s, garm, cot, btab, pg, pb, pc, isem, k_his, k_los, weights, bodies,
     send, recv, rsend, rrecv, tab3, gtgt, parts, stl, strv, far,
     ssem, rsem, rssem, rrsem, fsem, xsem, ysem, ready) = refs
    rows = 4 * cap
    outer_i, inner_i, frame_i = lax.axis_index("garm"), lax.axis_index("body"), lax.axis_index("frame")
    me = outer_i * inner + inner_i
    outer = owners // inner
    base = (outer - 2) * inner
    last = range(base + inner, owners)
    prior = range(base, base + inner)
    first_row, last_row, head = outer_i == 0, outer_i == outer - 1, me == 0

    def peer(k):
        p, bit = me, 1
        while bit < owners:
            p = p + ((k // bit) % 2) * (bit - 2 * bit * ((me // bit) % 2))
            bit *= 2
        return p

    def device(k):
        p = peer(k)
        return {"garm": p // inner, "body": p % inner}

    barrier = pltpu.get_barrier_semaphore()

    groups = [1 << b for b in range(owners.bit_length() - 1)]

    def below(bit):
        return (me // bit) % 2 == 1

    def over(first, count, cond, body):
        pl.when(cond)(lambda: each(count, lambda j: body(first + j)))

    def greet(k):
        pl.semaphore_signal(barrier, inc=1, device_id=device(k), device_id_type=MESH)

    def announce(k):
        pl.semaphore_signal(ready.at[k], inc=1, device_id=device(k), device_id_type=MESH)

    loads = [
        pltpu.make_async_copy(src, dst, isem.at[i])
        for i, (src, dst) in enumerate(zip(
            hbm, (garm, cot, btab.at[pl.ds(0, 3 * bb)], btab.at[pl.ds(3 * bb, bb)], pg, pb, pc)))]
    for load in loads:
        load.start()
    for bit in reversed(groups):
        over(bit, bit, jnp.logical_not(below(bit)), greet)
    pl.semaphore_signal(barrier, inc=1, device_id={"frame": 1 - frame_i}, device_id_type=MESH)

    for load in loads:
        load.wait()

    pl.semaphore_wait(barrier, me + 1)
    for bit in reversed(groups):
        over(bit, bit, below(bit), announce)

    lane = lax.broadcasted_iota(jnp.int32, (1, BLOCK), 1)
    lane_q = lane % rows // cap
    spread_row = lax.broadcasted_iota(jnp.int32, (16, 3 * BLOCK), 0)
    spread_lane = lax.broadcasted_iota(jnp.int32, (16, 3 * BLOCK), 1)
    spread_at = jnp.where(
        spread_lane < 2 * BLOCK, spread_lane // BLOCK * cap + spread_lane % cap, 2 * cap)
    spread = jnp.where(spread_row == spread_at, 1.0, 0.0).astype(BF)
    lists = jnp.concatenate(
        [pg[...], pb[...], pc[...], jnp.zeros((15 - 2 * cap, owners), jnp.int32)], axis=0)
    full = lax.dot_general(
        jnp.transpose(lists.astype(F32)).astype(BF), spread, (((1,), (0,)), ((), ())),
        preferred_element_type=F32)
    full_g = full[:, :BLOCK] + (lane_q * gb).astype(F32)
    full_b = full[:, BLOCK : 2 * BLOCK] + (lane_q * bb).astype(F32)
    live = jnp.where(
        (lane_q < 3) | ((lane % cap).astype(F32) < full[:, 2 * BLOCK :]), 1.0, 0.0)
    gtab = jnp.concatenate(
        split3(jnp.concatenate([garm[...] * SCALE, cot[...]], axis=0)), axis=0)
    own = lax.broadcasted_iota(jnp.int32, (GROUP, BLOCK), 0) == lane // rows
    wide_g = lax.broadcasted_iota(jnp.int32, (BLOCK, 12 * gb), 1) % (4 * gb)
    for u in range(owners // GROUP):
        here = slice(u * GROUP, (u + 1) * GROUP)
        targets = jnp.sum(jnp.where(own, full_g[here], 0.0), axis=0, keepdims=True)
        lives = jnp.sum(jnp.where(own, live[here], 0.0), axis=0, keepdims=True)
        gtgt[u] = targets
        turned = jnp.transpose(
            jnp.concatenate([targets, lives, jnp.zeros((6, BLOCK), F32)], axis=0))
        hot = jnp.where(wide_g == turned[:, 0:1].astype(jnp.int32), 1.0, 0.0).astype(BF)
        chosen = dot(hot, gtab) * turned[:, 1:2]
        for m in range(GROUP):
            send[u * GROUP + m, pl.ds(0, rows), :] = chosen[m * rows : (m + 1) * rows]
    for d in range(owners):
        send[d, pl.ds(rows, 1), :] = full_b[d : d + 1]

    def outgoing(k):
        return pltpu.make_async_remote_copy(
            src_ref=send.at[peer(k)], dst_ref=recv.at[me], send_sem=ssem.at[k], recv_sem=rsem.at[k],
            device_id=device(k), device_id_type=MESH)

    def returning(k):
        return pltpu.make_async_remote_copy(
            src_ref=rsend.at[peer(k)], dst_ref=rrecv.at[me], send_sem=rssem.at[k], recv_sem=rrsem.at[k],
            device_id=device(k), device_id_type=MESH)

    def table(rows_in):
        return jnp.concatenate(
            split3(jnp.concatenate([rows_in[: 3 * bb] * SCALE, rows_in[3 * bb :]], axis=0)), axis=0)

    def pushing(k):
        return pltpu.make_async_remote_copy(
            src_ref=btab, dst_ref=far.at[k - base], send_sem=xsem.at[k - base],
            recv_sem=ysem.at[k - base], device_id=device(k), device_id_type=MESH)

    tab3[...] = table(btab[...])

    row_id = lax.broadcasted_iota(jnp.int32, (rows, BLOCK), 0)
    row_c, place = row_id % cap, row_id < 3 * cap
    low_i, low_j = row_c < 2, row_c % 2 == 0
    wide = lax.broadcasted_iota(jnp.int32, (rows, 3 * 4 * bb), 1) % (4 * bb)
    slots = [jnp.concatenate([jnp.where(row_c == c, 1.0, 0.0).astype(BF)] * 6, axis=0) for c in range(cap)]

    def lhs(x, low):
        both = jnp.concatenate([jnp.where(low, x, 0.0), jnp.where(low, 0.0, x)], axis=1)
        return jnp.concatenate(split3(both), axis=0)

    def terms(x, scale):
        square = x[: 3 * cap] * x[: 3 * cap]
        norm = square[:cap] + square[cap : 2 * cap] + square[2 * cap :]
        full = jnp.concatenate([x[: 3 * cap] * scale, -norm], axis=0)
        hi = full.astype(BF).astype(F32)
        mid = (full - hi).astype(BF).astype(F32)
        low = full - hi - mid
        return [t.astype(BF) for t in (hi, mid, low, jnp.where(place, hi, 1.0), jnp.where(place, mid, 1.0))]

    def evaluate(got, row, tab):
        turned = jnp.transpose(jnp.concatenate([row, jnp.zeros((7, BLOCK), F32)], axis=0))
        onehot = jnp.where(wide == turned[:rows, 0:1].astype(jnp.int32), 1.0, 0.0).astype(BF)
        part = dot(onehot, tab)
        a1, a2, a3, a1o, a2o = terms(got, 1.0)
        b1, b2, b3, b1o, b2o = terms(part, 2.0)
        left = jnp.concatenate([a1, a2, a3, a2o, a1o, a1o], axis=0)
        right = jnp.concatenate([b1o, b2o, b1o, b1, b2, b3], axis=0)
        square = jnp.concatenate(
            [jnp.exp2(lax.dot_general(
                left, jnp.concatenate([right * slots[c], right * slots[c + 1]], axis=1),
                (((0,), (0,)), ((), ())), preferred_element_type=F32)) for c in (0, 2)], axis=0)
        k_hi = square.astype(BF)
        return part, k_hi, (square - k_hi.astype(F32)).astype(BF)

    def pull(got, part, k_hi, k_lo):
        cots = got[3 * cap :]
        stf = part[3 * cap :]
        lv = lhs(jnp.concatenate([jnp.concatenate([stf] * 3, axis=0) * part[: 3 * cap], stf], axis=0), low_j)
        rg = dot_t(lv, k_hi) + dot_t(lv, k_lo)
        rg = rg[:rows] + rg[rows : 2 * rows] + rg[2 * rows :]
        rg = jnp.where(low_i, rg[:, :BLOCK], rg[:, BLOCK:])
        sums = jnp.concatenate([rg[3 * cap :]] * 3, axis=0)
        cots3 = jnp.concatenate([cots] * 3, axis=0)
        return GRAD * (cots3 * (got[: 3 * cap] * sums - rg[: 3 * cap]))

    def process(k, got, row):
        part, k_hi, k_lo = evaluate(got, row, tab3[...])
        cots = got[3 * cap :]
        k_his[k], k_los[k] = k_hi, k_lo
        weights[k] = jnp.concatenate([jnp.concatenate([cots] * 3, axis=0) * got[: 3 * cap], cots], axis=0)
        bodies[k] = part
        return pull(got, part, k_hi, k_lo)

    def finish(k):
        part = bodies[k]
        lw = lhs(weights[k], low_i)
        rb = dot(lw, k_his[k]) + dot(lw, k_los[k])
        rb = rb[:rows] + rb[rows : 2 * rows] + rb[2 * rows :]
        rb = jnp.where(low_j, rb[:, :BLOCK], rb[:, BLOCK:])
        cols = rb[3 * cap :]
        cols3 = jnp.concatenate([cols] * 3, axis=0)
        stf3 = jnp.concatenate([part[3 * cap :]] * 3, axis=0)
        body_grad = GRAD * (stf3 * (part[: 3 * cap] * cols3 - rb[: 3 * cap]))
        parts[k] = jnp.concatenate([body_grad, amplitude * cols], axis=0)

    for bit in reversed(groups):
        over(bit, bit, below(bit), lambda k: outgoing(k).start())

    def push_last():
        for k in last:
            pushing(k).start()

    def push_prior():
        pushing(me).start()

    pl.when(last_row)(push_last)
    pl.when(outer_i == outer - 2)(push_prior)

    def raise_to(first, count, bit):
        def one(k):
            pl.semaphore_wait(ready.at[k], 1)
            outgoing(k).start()

        over(first, count, jnp.logical_not(below(bit)), one)

    recv[me, pl.ds(rows, 1), :] = send[me, pl.ds(rows, 1), :]
    rrecv[me] = process(me, send[me, pl.ds(0, rows), :], send[me, pl.ds(rows, 1), :])


    def returns(k):
        if not isinstance(k, int):
            here = jnp.logical_or(k < base, jnp.logical_and(k < base + inner, me != k))
            return jnp.logical_or(here, jnp.logical_and(k >= base + inner, jnp.logical_not(last_row)))
        return True if k < base else (me != k if k in prior else jnp.logical_not(last_row))

    def when(cond, body):
        if cond is True:
            body()
        else:
            pl.when(cond)(body)

    def arrive(ks):
        for k in ks:
            outgoing(k).wait_recv()
        grads = [process(peer(k), recv[peer(k), pl.ds(0, rows), :], recv[peer(k), pl.ds(rows, 1), :])
                 for k in ks]
        for k, grad in zip(ks, grads):
            rsend[peer(k)] = grad
        for k in ks:
            when(returns(k), lambda k=k: returning(k).start())

    for bit in groups[:-1]:
        raise_to(bit, bit, bit)
    raise_to(owners // 2, base + inner - owners // 2, owners // 2)
    arrive([1])
    raise_to(base + inner, inner, owners // 2)
    each(owners // 2 - 1, lambda j: arrive([2 * j + 2, 2 * j + 3]))

    def fetch(ks):
        for k in ks:
            pushing(k).wait_recv()
        done = []
        for k in ks:
            got, row = send[peer(k), pl.ds(0, rows), :], send[peer(k), pl.ds(rows, 1), :]
            done.append(pull(got, *evaluate(got, row, table(far[k - base]))))
        for k, grad in zip(ks, done):
            rrecv[peer(k)] = grad

    each(owners, finish)

    def scatter(height, target_row, values):
        hot = jnp.where(
            lax.broadcasted_iota(jnp.int32, (height, BLOCK), 0) == target_row, 1.0, 0.0).astype(BF)
        hi, mid, lo = split3(values)
        return dot(jnp.concatenate([hot, hot, hot], axis=1), jnp.concatenate([hi, mid, lo], axis=0))

    def over_groups(one):
        total = one(0)
        for u in range(1, owners // GROUP):
            total = total + one(u)
        return total

    def body_group(u):
        target = jnp.zeros((1, BLOCK), F32)
        for m in range(GROUP):
            target = jnp.where(lane // rows == m, recv[u * GROUP + m, pl.ds(rows, 1), :], target)
        return scatter(4 * bb, target.astype(jnp.int32),
                       jnp.concatenate([parts[u * GROUP + m] for m in range(GROUP)], axis=0))

    body_sum = over_groups(body_group)
    stl[...] = body_sum[3 * bb :]
    stiff_copy = pltpu.make_async_remote_copy(
        src_ref=stl, dst_ref=strv, send_sem=fsem.at[0], recv_sem=fsem.at[1],
        device_id={"frame": 1 - frame_i}, device_id_type=MESH)
    stiff_copy.start()
    out_b[...] = body_sum[: 3 * bb]
    pl.when(head)(lambda: fetch([*prior, *last]))
    pl.when(jnp.logical_and(first_row, jnp.logical_not(head)))(lambda: fetch(last))
    each(owners - 1, lambda j: outgoing(j + 1).wait_send())
    stiff_copy.wait()
    out_s[...] = stl[...] + strv[...]
    each(base - 1, lambda j: returning(j + 1).wait_recv())

    def await_returns(ks):
        for k in ks:
            returning(k).wait_recv()

    pl.when(jnp.logical_not(head))(lambda: await_returns(prior))
    pl.when(jnp.logical_not(first_row))(lambda: await_returns(last))

    def garm_group(u):
        blank = jnp.zeros((cap, BLOCK), F32)
        pieces = []
        for m in range(GROUP):
            pieces += [rrecv[u * GROUP + m], blank]
        return scatter(3 * gb, gtgt[u].astype(jnp.int32), jnp.concatenate(pieces, axis=0))

    out_g[...] = over_groups(garm_group)
    each(owners - 1, lambda j: when(returns(j + 1), lambda: returning(j + 1).wait_send()))

    def settle_last():
        for k in last:
            pushing(k).wait_send()

    def settle_prior():
        pushing(me).wait_send()

    pl.when(last_row)(settle_last)
    pl.when(outer_i == outer - 2)(settle_prior)


def write_out(*refs):
    copies = [pltpu.make_async_copy(refs[i], refs[3 + i], refs[6].at[i]) for i in range(3)]
    for copy in copies:
        copy.start()
    for copy in copies:
        copy.wait()


def per_device(owners, inner, garment, cotangent, body_points, stiffness, pair_garment, pair_body, pair_count):
    cap = pair_garment.shape[3]
    gb, bb = garment.shape[2] // BLOCK, body_points.shape[2] // BLOCK
    rows = 4 * cap
    vmem = pl.BlockSpec(memory_space=pltpu.VMEM)
    out_g, out_b, out_s = pl.pallas_call(
        functools.partial(kernel, owners, inner, cap, gb, bb),
        out_shape=(
            jax.ShapeDtypeStruct((3 * gb, BLOCK), F32),
            jax.ShapeDtypeStruct((3 * bb, BLOCK), F32),
            jax.ShapeDtypeStruct((bb, BLOCK), F32),
        ),
        in_specs=[pl.BlockSpec(memory_space=pltpu.HBM)] * 7,
        out_specs=[vmem] * 3,
        scratch_shapes=[
            pltpu.VMEM((3 * gb, BLOCK), F32),
            pltpu.VMEM((gb, BLOCK), F32),
            pltpu.VMEM((4 * bb, BLOCK), F32),
            pltpu.VMEM((cap, owners), jnp.int32),
            pltpu.VMEM((cap, owners), jnp.int32),
            pltpu.VMEM((1, owners), jnp.int32),
            pltpu.SemaphoreType.DMA((7,)),
            pltpu.VMEM((owners, 2 * BLOCK, 2 * BLOCK), BF),
            pltpu.VMEM((owners, 2 * BLOCK, 2 * BLOCK), BF),
            pltpu.VMEM((owners, rows, BLOCK), F32),
            pltpu.VMEM((owners, rows, BLOCK), F32),
            pltpu.VMEM((owners, rows + 1, BLOCK), F32),
            pltpu.VMEM((owners, rows + 1, BLOCK), F32),
            pltpu.VMEM((owners, 3 * cap, BLOCK), F32),
            pltpu.VMEM((owners, 3 * cap, BLOCK), F32),
            pltpu.VMEM((3 * 4 * bb, BLOCK), BF),
            pltpu.VMEM((owners // GROUP, 1, BLOCK), F32),
            pltpu.VMEM((owners, rows, BLOCK), F32),
            pltpu.VMEM((bb, BLOCK), F32),
            pltpu.VMEM((bb, BLOCK), F32),
            pltpu.VMEM((2 * inner, 4 * bb, BLOCK), F32),
            pltpu.SemaphoreType.DMA((owners,)),
            pltpu.SemaphoreType.DMA((owners,)),
            pltpu.SemaphoreType.DMA((owners,)),
            pltpu.SemaphoreType.DMA((owners,)),
            pltpu.SemaphoreType.DMA((2,)),
            pltpu.SemaphoreType.DMA((2 * inner,)),
            pltpu.SemaphoreType.DMA((2 * inner,)),
            pltpu.SemaphoreType.REGULAR((owners,)),
        ],
        compiler_params=pltpu.CompilerParams(collective_id=0, has_side_effects=True,
            vmem_limit_bytes=(8 * 2**20 + owners * 5 * 2**16)),
        name="contact",
    )(
        pltpu.with_memory_space_constraint(garment.reshape(3 * gb, BLOCK), pltpu.HBM),
        pltpu.with_memory_space_constraint(cotangent.reshape(gb, BLOCK), pltpu.HBM),
        pltpu.with_memory_space_constraint(body_points.reshape(3 * bb, BLOCK), pltpu.HBM),
        pltpu.with_memory_space_constraint(stiffness.reshape(bb, BLOCK), pltpu.HBM),
        pltpu.with_memory_space_constraint(pair_garment.reshape(owners, cap).T, pltpu.HBM),
        pltpu.with_memory_space_constraint(pair_body.reshape(owners, cap).T, pltpu.HBM),
        pltpu.with_memory_space_constraint(pair_count.reshape(1, owners), pltpu.HBM),
    )
    out_g, out_b, out_s = pl.pallas_call(
        write_out,
        out_shape=tuple(jax.ShapeDtypeStruct(o.shape, o.dtype) for o in (out_g, out_b, out_s)),
        in_specs=[vmem] * 3,
        out_specs=[pl.BlockSpec(memory_space=pltpu.HBM)] * 3,
        scratch_shapes=[pltpu.SemaphoreType.DMA((3,))],
        compiler_params=pltpu.CompilerParams(vmem_limit_bytes=2**20),
        name="write_out",
    )(out_g, out_b, out_s)
    return (
        out_g.reshape(1, 3, gb * BLOCK),
        out_b.reshape(1, 3, bb * BLOCK),
        out_s.reshape(bb * BLOCK),
    )


def solution(mesh):
    inner = mesh.shape["body"]
    owners = mesh.shape["garm"] * inner
    in_specs = (
        P(("grp", "frame"), None, ("garm", "body")),
        P(("grp", "frame"), ("garm", "body")),
        P(("grp", "frame"), None, ("garm", "body")),
        P(("grp", "garm", "body")),
        P(("grp", "frame"), ("garm", "body"), None, None),
        P(("grp", "frame"), ("garm", "body"), None, None),
        P(("grp", "frame"), ("garm", "body"), None),
    )
    out_specs = (
        P(("grp", "frame"), None, ("garm", "body")),
        P(("grp", "frame"), None, ("garm", "body")),
        P(("grp", "garm", "body")),
    )
    return jax.shard_map(
        functools.partial(per_device, owners, inner),
        mesh=mesh, in_specs=in_specs, out_specs=out_specs, check_vma=False)
```

```python
import functools
import math

import jax
import jax.numpy as jnp
from jax import lax
from jax.experimental import pallas as pl
from jax.experimental.pallas import tpu as pltpu
from jax.sharding import PartitionSpec as P

BLOCK = 128
amplitude = 0.05
width_sq = 4.0
SCALE = math.sqrt(math.log2(math.e) / width_sq)
GRAD = -2.0 / width_sq * amplitude / SCALE
GROUP = 8
MESH = pl.DeviceIdType.MESH
BF = jnp.bfloat16
F32 = jnp.float32


def split3(v):
    hi = v.astype(BF)
    rest = v - hi.astype(F32)
    mid = rest.astype(BF)
    return hi, mid, (rest - mid.astype(F32)).astype(BF)


def dot(a, b):
    return jnp.dot(a, b, preferred_element_type=F32)


def dot_t(a, b):
    return lax.dot_general(a, b, (((1,), (1,)), ((), ())), preferred_element_type=F32)


def each(count, body):
    if count <= 8:
        for k in range(count):
            body(k)
    else:
        lax.fori_loop(0, count, lambda k, c: (body(k), c)[1], 0)


def kernel(owners, inner, cap, gb, bb, *refs):
    hbm, refs = refs[:7], refs[7:]
    (out_g, out_b, out_s, garm, cot, btab, pg, pb, pc, isem, k_his, k_los, weights, bodies,
     send, recv, rsend, rrecv, tab3, gtgt, parts, stl, strv, far,
     ssem, rsem, rssem, rrsem, fsem, xsem, ysem, ready) = refs
    rows = 4 * cap
    outer_i, inner_i, frame_i = lax.axis_index("garm"), lax.axis_index("body"), lax.axis_index("frame")
    me = outer_i * inner + inner_i
    outer = owners // inner
    base = (outer - 2) * inner
    last = range(base + inner, owners)
    prior = range(base, base + inner)
    first_row, last_row, head = outer_i == 0, outer_i == outer - 1, me == 0

    def peer(k):
        p, bit = me, 1
        while bit < owners:
            p = p + ((k // bit) % 2) * (bit - 2 * bit * ((me // bit) % 2))
            bit *= 2
        return p

    def device(k):
        p = peer(k)
        return {"garm": p // inner, "body": p % inner}

    barrier = pltpu.get_barrier_semaphore()

    groups = [1 << b for b in range(owners.bit_length() - 1)]

    def below(bit):
        return (me // bit) % 2 == 1

    def over(first, count, cond, body):
        pl.when(cond)(lambda: each(count, lambda j: body(first + count - 1 - j)))

    def greet(k):
        pl.semaphore_signal(barrier, inc=1, device_id=device(k), device_id_type=MESH)

    def announce(k):
        pl.semaphore_signal(ready.at[k], inc=1, device_id=device(k), device_id_type=MESH)

    loads = [
        pltpu.make_async_copy(src, dst, isem.at[i])
        for i, (src, dst) in enumerate(zip(
            hbm, (garm, cot, btab.at[pl.ds(0, 3 * bb)], btab.at[pl.ds(3 * bb, bb)], pg, pb, pc)))]
    for load in loads[4:] + loads[:4]:
        load.start()
    for bit in reversed(groups):
        over(bit, bit, jnp.logical_not(below(bit)), greet)
    pl.semaphore_signal(barrier, inc=1, device_id={"frame": 1 - frame_i}, device_id_type=MESH)

    def meet():
        pl.semaphore_wait(barrier, me + 1)
        for bit in reversed(groups):
            over(bit, bit, below(bit), announce)

    pl.when(inner_i == inner - 1)(meet)
    for load in loads[4:]:
        load.wait()

    lane = lax.broadcasted_iota(jnp.int32, (1, BLOCK), 1)
    lane_q = lane % rows // cap
    spread_row = lax.broadcasted_iota(jnp.int32, (16, 3 * BLOCK), 0)
    spread_lane = lax.broadcasted_iota(jnp.int32, (16, 3 * BLOCK), 1)
    spread_at = jnp.where(
        spread_lane < 2 * BLOCK, spread_lane // BLOCK * cap + spread_lane % cap, 2 * cap)
    spread = jnp.where(spread_row == spread_at, 1.0, 0.0).astype(BF)
    lists = jnp.concatenate(
        [pg[...], pb[...], pc[...], jnp.zeros((15 - 2 * cap, owners), jnp.int32)], axis=0)
    full = lax.dot_general(
        jnp.transpose(lists.astype(F32)).astype(BF), spread, (((1,), (0,)), ((), ())),
        preferred_element_type=F32)
    full_g = full[:, :BLOCK] + (lane_q * gb).astype(F32)
    full_b = full[:, BLOCK : 2 * BLOCK] + (lane_q * bb).astype(F32)
    live = jnp.where(
        (lane_q < 3) | ((lane % cap).astype(F32) < full[:, 2 * BLOCK :]), 1.0, 0.0)
    own = lax.broadcasted_iota(jnp.int32, (GROUP, BLOCK), 0) == lane // rows
    wide_g = lax.broadcasted_iota(jnp.int32, (BLOCK, 12 * gb), 1) % (4 * gb)
    picks = []
    for u in range(owners // GROUP):
        here = slice(u * GROUP, (u + 1) * GROUP)
        targets = jnp.sum(jnp.where(own, full_g[here], 0.0), axis=0, keepdims=True)
        lives = jnp.sum(jnp.where(own, live[here], 0.0), axis=0, keepdims=True)
        gtgt[u] = targets
        turned = jnp.transpose(
            jnp.concatenate([targets, lives, jnp.zeros((6, BLOCK), F32)], axis=0))
        picks.append((jnp.where(wide_g == turned[:, 0:1].astype(jnp.int32), 1.0, 0.0).astype(BF), turned[:, 1:2]))
    for d in range(owners):
        send[d, pl.ds(rows, 1), :] = full_b[d : d + 1]

    pl.when(inner_i < inner - 1)(meet)
    for load in loads[:2]:
        load.wait()
    gtab = jnp.concatenate(
        split3(jnp.concatenate([garm[...] * SCALE, cot[...]], axis=0)), axis=0)
    for u, (hot, lives) in enumerate(picks):
        chosen = dot(hot, gtab) * lives
        for m in range(GROUP):
            send[u * GROUP + m, pl.ds(0, rows), :] = chosen[m * rows : (m + 1) * rows]

    def outgoing(k):
        return pltpu.make_async_remote_copy(
            src_ref=send.at[peer(k)], dst_ref=recv.at[me], send_sem=ssem.at[k], recv_sem=rsem.at[k],
            device_id=device(k), device_id_type=MESH)

    def returning(k):
        return pltpu.make_async_remote_copy(
            src_ref=rsend.at[peer(k)], dst_ref=rrecv.at[me], send_sem=rssem.at[k], recv_sem=rrsem.at[k],
            device_id=device(k), device_id_type=MESH)

    def table(rows_in):
        return jnp.concatenate(
            split3(jnp.concatenate([rows_in[: 3 * bb] * SCALE, rows_in[3 * bb :]], axis=0)), axis=0)

    def pushing(k):
        return pltpu.make_async_remote_copy(
            src_ref=btab, dst_ref=far.at[k - base], send_sem=xsem.at[k - base],
            recv_sem=ysem.at[k - base], device_id=device(k), device_id_type=MESH)


    row_id = lax.broadcasted_iota(jnp.int32, (rows, BLOCK), 0)
    row_c, place = row_id % cap, row_id < 3 * cap
    low_i, low_j = row_c < 2, row_c % 2 == 0
    wide = lax.broadcasted_iota(jnp.int32, (rows, 3 * 4 * bb), 1) % (4 * bb)
    slots = [jnp.concatenate([jnp.where(row_c == c, 1.0, 0.0).astype(BF)] * 6, axis=0) for c in range(cap)]

    def lhs(x, low):
        both = jnp.concatenate([jnp.where(low, x, 0.0), jnp.where(low, 0.0, x)], axis=1)
        return jnp.concatenate(split3(both), axis=0)

    def terms(x, scale):
        square = x[: 3 * cap] * x[: 3 * cap]
        norm = square[:cap] + square[cap : 2 * cap] + square[2 * cap :]
        full = jnp.concatenate([x[: 3 * cap] * scale, -norm], axis=0)
        hi = full.astype(BF).astype(F32)
        mid = (full - hi).astype(BF).astype(F32)
        low = full - hi - mid
        return [t.astype(BF) for t in (hi, mid, low, jnp.where(place, hi, 1.0), jnp.where(place, mid, 1.0))]

    def evaluate(got, row, tab):
        turned = jnp.transpose(jnp.concatenate([row, jnp.zeros((7, BLOCK), F32)], axis=0))
        onehot = jnp.where(wide == turned[:rows, 0:1].astype(jnp.int32), 1.0, 0.0).astype(BF)
        part = dot(onehot, tab)
        a1, a2, a3, a1o, a2o = terms(got, 1.0)
        b1, b2, b3, b1o, b2o = terms(part, 2.0)
        left = jnp.concatenate([a1, a2, a3, a2o, a1o, a1o], axis=0)
        right = jnp.concatenate([b1o, b2o, b1o, b1, b2, b3], axis=0)
        square = jnp.concatenate(
            [jnp.exp2(lax.dot_general(
                left, jnp.concatenate([right * slots[c], right * slots[c + 1]], axis=1),
                (((0,), (0,)), ((), ())), preferred_element_type=F32)) for c in (0, 2)], axis=0)
        k_hi = square.astype(BF)
        return part, k_hi, (square - k_hi.astype(F32)).astype(BF)

    def pull(got, part, k_hi, k_lo):
        cots = got[3 * cap :]
        stf = part[3 * cap :]
        lv = lhs(jnp.concatenate([jnp.concatenate([stf] * 3, axis=0) * part[: 3 * cap], stf], axis=0), low_j)
        rg = dot_t(lv, k_hi) + dot_t(lv, k_lo)
        rg = rg[:rows] + rg[rows : 2 * rows] + rg[2 * rows :]
        rg = jnp.where(low_i, rg[:, :BLOCK], rg[:, BLOCK:])
        sums = jnp.concatenate([rg[3 * cap :]] * 3, axis=0)
        cots3 = jnp.concatenate([cots] * 3, axis=0)
        return GRAD * (cots3 * (got[: 3 * cap] * sums - rg[: 3 * cap]))

    def process(k, got, row):
        part, k_hi, k_lo = evaluate(got, row, tab3[...])
        cots = got[3 * cap :]
        k_his[k], k_los[k] = k_hi, k_lo
        weights[k] = jnp.concatenate([jnp.concatenate([cots] * 3, axis=0) * got[: 3 * cap], cots], axis=0)
        bodies[k] = part
        return pull(got, part, k_hi, k_lo)

    def finish(k):
        part = bodies[k]
        lw = lhs(weights[k], low_i)
        rb = dot(lw, k_his[k]) + dot(lw, k_los[k])
        rb = rb[:rows] + rb[rows : 2 * rows] + rb[2 * rows :]
        rb = jnp.where(low_j, rb[:, :BLOCK], rb[:, BLOCK:])
        cols = rb[3 * cap :]
        cols3 = jnp.concatenate([cols] * 3, axis=0)
        stf3 = jnp.concatenate([part[3 * cap :]] * 3, axis=0)
        body_grad = GRAD * (stf3 * (part[: 3 * cap] * cols3 - rb[: 3 * cap]))
        parts[k] = jnp.concatenate([body_grad, amplitude * cols], axis=0)

    for bit in reversed(groups):
        pl.when(below(bit))(lambda bit=bit: each(bit, lambda j: outgoing(bit + j).start()))
    for load in loads[2:4]:
        load.wait()
    tab3[...] = table(btab[...])

    def push_last():
        for k in last:
            pushing(k).start()

    def push_prior():
        pushing(me).start()

    pl.when(outer_i == outer - 2)(push_prior)

    def raise_to(first, count, bit):
        def one(j):
            pl.semaphore_wait(ready.at[first + j], 1)
            outgoing(first + j).start()

        pl.when(jnp.logical_not(below(bit)))(lambda: each(count, one))

    recv[me, pl.ds(rows, 1), :] = send[me, pl.ds(rows, 1), :]
    rrecv[me] = process(me, send[me, pl.ds(0, rows), :], send[me, pl.ds(rows, 1), :])

    pl.when(last_row)(push_last)


    def returns(k):
        if not isinstance(k, int):
            here = jnp.logical_or(k < base, jnp.logical_and(k < base + inner, me != k))
            return jnp.logical_or(here, jnp.logical_and(k >= base + inner, jnp.logical_not(last_row)))
        return True if k < base else (me != k if k in prior else jnp.logical_not(last_row))

    def when(cond, body):
        if cond is True:
            body()
        else:
            pl.when(cond)(body)

    def arrive(ks):
        for k in ks:
            outgoing(k).wait_recv()
        grads = [process(peer(k), recv[peer(k), pl.ds(0, rows), :], recv[peer(k), pl.ds(rows, 1), :])
                 for k in ks]
        for k, grad in zip(ks, grads):
            rsend[peer(k)] = grad
        for k in ks:
            when(returns(k), lambda k=k: returning(k).start())

    for bit in groups[:-1]:
        raise_to(bit, bit, bit)
    half = owners // 2
    odd = below(half // 2)
    pl.when(odd)(lambda: raise_to(half + half // 2, half // 2, half))
    raise_to(half, half // 2, half)
    arrive([1])
    pl.when(jnp.logical_not(odd))(lambda: raise_to(half + half // 2, half // 2, half))
    each(owners // 2 - 1, lambda j: arrive([2 * j + 2, 2 * j + 3]))

    def fetch(ks):
        for k in ks:
            pushing(k).wait_recv()
        done = []
        for k in ks:
            got, row = send[peer(k), pl.ds(0, rows), :], send[peer(k), pl.ds(rows, 1), :]
            done.append(pull(got, *evaluate(got, row, table(far[k - base]))))
        for k, grad in zip(ks, done):
            rrecv[peer(k)] = grad

    each(owners, finish)

    def scatter(height, target_row, values):
        hot = jnp.where(
            lax.broadcasted_iota(jnp.int32, (height, BLOCK), 0) == target_row, 1.0, 0.0).astype(BF)
        hi, mid, lo = split3(values)
        return dot(jnp.concatenate([hot, hot, hot], axis=1), jnp.concatenate([hi, mid, lo], axis=0))

    def over_groups(one):
        total = one(0)
        for u in range(1, owners // GROUP):
            total = total + one(u)
        return total

    def body_group(u):
        target = jnp.zeros((1, BLOCK), F32)
        for m in range(GROUP):
            target = jnp.where(lane // rows == m, recv[u * GROUP + m, pl.ds(rows, 1), :], target)
        return scatter(4 * bb, target.astype(jnp.int32),
                       jnp.concatenate([parts[u * GROUP + m] for m in range(GROUP)], axis=0))

    body_sum = over_groups(body_group)
    stl[...] = body_sum[3 * bb :]
    stiff_copy = pltpu.make_async_remote_copy(
        src_ref=stl, dst_ref=strv, send_sem=fsem.at[0], recv_sem=fsem.at[1],
        device_id={"frame": 1 - frame_i}, device_id_type=MESH)
    stiff_copy.start()
    out_b[...] = body_sum[: 3 * bb]
    pl.when(head)(lambda: fetch([*prior, *last]))
    pl.when(jnp.logical_and(first_row, jnp.logical_not(head)))(lambda: fetch(last))
    each(owners - 1, lambda j: outgoing(j + 1).wait_send())
    stiff_copy.wait()
    out_s[...] = stl[...] + strv[...]
    each(base - 1, lambda j: returning(j + 1).wait_recv())

    def await_returns(ks):
        for k in ks:
            returning(k).wait_recv()

    pl.when(jnp.logical_not(head))(lambda: await_returns(prior))
    pl.when(jnp.logical_not(first_row))(lambda: await_returns(last))

    def garm_group(u):
        blank = jnp.zeros((cap, BLOCK), F32)
        pieces = []
        for m in range(GROUP):
            pieces += [rrecv[u * GROUP + m], blank]
        return scatter(3 * gb, gtgt[u].astype(jnp.int32), jnp.concatenate(pieces, axis=0))

    out_g[...] = over_groups(garm_group)
    each(owners - 1, lambda j: when(returns(j + 1), lambda: returning(j + 1).wait_send()))

    def settle_last():
        for k in last:
            pushing(k).wait_send()

    def settle_prior():
        pushing(me).wait_send()

    pl.when(last_row)(settle_last)
    pl.when(outer_i == outer - 2)(settle_prior)


def write_out(*refs):
    copies = [pltpu.make_async_copy(refs[i], refs[3 + i], refs[6].at[i]) for i in range(3)]
    for copy in copies:
        copy.start()
    for copy in copies:
        copy.wait()


def per_device(owners, inner, garment, cotangent, body_points, stiffness, pair_garment, pair_body, pair_count):
    cap = pair_garment.shape[3]
    gb, bb = garment.shape[2] // BLOCK, body_points.shape[2] // BLOCK
    rows = 4 * cap
    vmem = pl.BlockSpec(memory_space=pltpu.VMEM)
    out_g, out_b, out_s = pl.pallas_call(
        functools.partial(kernel, owners, inner, cap, gb, bb),
        out_shape=(
            jax.ShapeDtypeStruct((3 * gb, BLOCK), F32),
            jax.ShapeDtypeStruct((3 * bb, BLOCK), F32),
            jax.ShapeDtypeStruct((bb, BLOCK), F32),
        ),
        in_specs=[pl.BlockSpec(memory_space=pltpu.HBM)] * 7,
        out_specs=[vmem] * 3,
        scratch_shapes=[
            pltpu.VMEM((3 * gb, BLOCK), F32),
            pltpu.VMEM((gb, BLOCK), F32),
            pltpu.VMEM((4 * bb, BLOCK), F32),
            pltpu.VMEM((cap, owners), jnp.int32),
            pltpu.VMEM((cap, owners), jnp.int32),
            pltpu.VMEM((1, owners), jnp.int32),
            pltpu.SemaphoreType.DMA((7,)),
            pltpu.VMEM((owners, 2 * BLOCK, 2 * BLOCK), BF),
            pltpu.VMEM((owners, 2 * BLOCK, 2 * BLOCK), BF),
            pltpu.VMEM((owners, rows, BLOCK), F32),
            pltpu.VMEM((owners, rows, BLOCK), F32),
            pltpu.VMEM((owners, rows + 1, BLOCK), F32),
            pltpu.VMEM((owners, rows + 1, BLOCK), F32),
            pltpu.VMEM((owners, 3 * cap, BLOCK), F32),
            pltpu.VMEM((owners, 3 * cap, BLOCK), F32),
            pltpu.VMEM((3 * 4 * bb, BLOCK), BF),
            pltpu.VMEM((owners // GROUP, 1, BLOCK), F32),
            pltpu.VMEM((owners, rows, BLOCK), F32),
            pltpu.VMEM((bb, BLOCK), F32),
            pltpu.VMEM((bb, BLOCK), F32),
            pltpu.VMEM((2 * inner, 4 * bb, BLOCK), F32),
            pltpu.SemaphoreType.DMA((owners,)),
            pltpu.SemaphoreType.DMA((owners,)),
            pltpu.SemaphoreType.DMA((owners,)),
            pltpu.SemaphoreType.DMA((owners,)),
            pltpu.SemaphoreType.DMA((2,)),
            pltpu.SemaphoreType.DMA((2 * inner,)),
            pltpu.SemaphoreType.DMA((2 * inner,)),
            pltpu.SemaphoreType.REGULAR((owners,)),
        ],
        compiler_params=pltpu.CompilerParams(collective_id=0, has_side_effects=True,
            vmem_limit_bytes=(8 * 2**20 + owners * 5 * 2**16)),
        name="contact",
    )(
        pltpu.with_memory_space_constraint(garment.reshape(3 * gb, BLOCK), pltpu.HBM),
        pltpu.with_memory_space_constraint(cotangent.reshape(gb, BLOCK), pltpu.HBM),
        pltpu.with_memory_space_constraint(body_points.reshape(3 * bb, BLOCK), pltpu.HBM),
        pltpu.with_memory_space_constraint(stiffness.reshape(bb, BLOCK), pltpu.HBM),
        pltpu.with_memory_space_constraint(pair_garment.reshape(owners, cap).T, pltpu.HBM),
        pltpu.with_memory_space_constraint(pair_body.reshape(owners, cap).T, pltpu.HBM),
        pltpu.with_memory_space_constraint(pair_count.reshape(1, owners), pltpu.HBM),
    )
    out_g, out_b, out_s = pl.pallas_call(
        write_out,
        out_shape=tuple(jax.ShapeDtypeStruct(o.shape, o.dtype) for o in (out_g, out_b, out_s)),
        in_specs=[vmem] * 3,
        out_specs=[pl.BlockSpec(memory_space=pltpu.HBM)] * 3,
        scratch_shapes=[pltpu.SemaphoreType.DMA((3,))],
        compiler_params=pltpu.CompilerParams(vmem_limit_bytes=2**20),
        name="write_out",
    )(out_g, out_b, out_s)
    return (
        out_g.reshape(1, 3, gb * BLOCK),
        out_b.reshape(1, 3, bb * BLOCK),
        out_s.reshape(bb * BLOCK),
    )


def solution(mesh):
    inner = mesh.shape["body"]
    owners = mesh.shape["garm"] * inner
    in_specs = (
        P(("grp", "frame"), None, ("garm", "body")),
        P(("grp", "frame"), ("garm", "body")),
        P(("grp", "frame"), None, ("garm", "body")),
        P(("grp", "garm", "body")),
        P(("grp", "frame"), ("garm", "body"), None, None),
        P(("grp", "frame"), ("garm", "body"), None, None),
        P(("grp", "frame"), ("garm", "body"), None),
    )
    out_specs = (
        P(("grp", "frame"), None, ("garm", "body")),
        P(("grp", "frame"), None, ("garm", "body")),
        P(("grp", "garm", "body")),
    )
    return jax.shard_map(
        functools.partial(per_device, owners, inner),
        mesh=mesh, in_specs=in_specs, out_specs=out_specs, check_vma=False)
```

```python
import functools
import math

import jax
import jax.numpy as jnp
from jax import lax
from jax.experimental import pallas as pl
from jax.experimental.pallas import tpu as pltpu
from jax.sharding import PartitionSpec as P

BLOCK = 128
amplitude = 0.05
width_sq = 4.0
SCALE = math.sqrt(math.log2(math.e) / width_sq)
GRAD = -2.0 / width_sq * amplitude / SCALE
GROUP = 8
MESH = pl.DeviceIdType.MESH
BF = jnp.bfloat16
F32 = jnp.float32


def split3(v):
    hi = v.astype(BF)
    rest = v - hi.astype(F32)
    mid = rest.astype(BF)
    return hi, mid, (rest - mid.astype(F32)).astype(BF)


def dot(a, b):
    return jnp.dot(a, b, preferred_element_type=F32)


def dot_t(a, b):
    return lax.dot_general(a, b, (((1,), (1,)), ((), ())), preferred_element_type=F32)


def each(count, body):
    if count <= 8:
        for k in range(count):
            body(k)
    else:
        lax.fori_loop(0, count, lambda k, c: (body(k), c)[1], 0)


def kernel(owners, inner, cap, gb, bb, *refs):
    hbm, refs = refs[:7], refs[7:]
    (out_g, out_b, out_s, garm, cot, btab, pg, pb, pc, isem, k_his, k_los, weights, bodies,
     send, recv, rsend, rrecv, tab3, gtgt, parts, stl, strv, far,
     ssem, rsem, rssem, rrsem, fsem, xsem, ysem, ready) = refs
    rows = 4 * cap
    outer_i, inner_i, frame_i = lax.axis_index("garm"), lax.axis_index("body"), lax.axis_index("frame")
    me = outer_i * inner + inner_i
    outer = owners // inner
    base = (outer - 2) * inner
    last = range(base + inner, owners)
    prior = range(base, base + inner)
    first_row, last_row, head = outer_i == 0, outer_i == outer - 1, me == 0

    def peer(k):
        p, bit = me, 1
        while bit < owners:
            p = p + ((k // bit) % 2) * (bit - 2 * bit * ((me // bit) % 2))
            bit *= 2
        return p

    def device(k):
        p = peer(k)
        return {"garm": p // inner, "body": p % inner}

    barrier = pltpu.get_barrier_semaphore()

    groups = [1 << b for b in range(owners.bit_length() - 1)]

    def below(bit):
        return (me // bit) % 2 == 1

    def over(first, count, cond, body):
        pl.when(cond)(lambda: each(count, lambda j: body(first + count - 1 - j)))

    def greet(k):
        pl.semaphore_signal(barrier, inc=1, device_id=device(k), device_id_type=MESH)

    def announce(k):
        pl.semaphore_signal(ready.at[k], inc=1, device_id=device(k), device_id_type=MESH)

    loads = [
        pltpu.make_async_copy(src, dst, isem.at[i])
        for i, (src, dst) in enumerate(zip(
            hbm, (garm, cot, btab.at[pl.ds(0, 3 * bb)], btab.at[pl.ds(3 * bb, bb)], pg, pb, pc)))]
    for load in loads[4:] + loads[:4]:
        load.start()
    for bit in reversed(groups):
        over(bit, bit, jnp.logical_not(below(bit)), greet)
    pl.semaphore_signal(barrier, inc=1, device_id={"frame": 1 - frame_i}, device_id_type=MESH)

    def meet():
        pl.semaphore_wait(barrier, me + 1)
        for bit in reversed(groups):
            over(bit, bit, below(bit), announce)

    pl.when(inner_i == inner - 1)(meet)
    for load in loads[4:]:
        load.wait()

    lane = lax.broadcasted_iota(jnp.int32, (1, BLOCK), 1)
    lane_q = lane % rows // cap
    spread_row = lax.broadcasted_iota(jnp.int32, (16, 3 * BLOCK), 0)
    spread_lane = lax.broadcasted_iota(jnp.int32, (16, 3 * BLOCK), 1)
    spread_at = jnp.where(
        spread_lane < 2 * BLOCK, spread_lane // BLOCK * cap + spread_lane % cap, 2 * cap)
    spread = jnp.where(spread_row == spread_at, 1.0, 0.0).astype(BF)
    lists = jnp.concatenate(
        [pg[...], pb[...], pc[...], jnp.zeros((15 - 2 * cap, owners), jnp.int32)], axis=0)
    full = lax.dot_general(
        jnp.transpose(lists.astype(F32)).astype(BF), spread, (((1,), (0,)), ((), ())),
        preferred_element_type=F32)
    full_g = full[:, :BLOCK] + (lane_q * gb).astype(F32)
    full_b = full[:, BLOCK : 2 * BLOCK] + (lane_q * bb).astype(F32)
    own = lax.broadcasted_iota(jnp.int32, (GROUP, BLOCK), 0) == lane // rows
    wide_g = lax.broadcasted_iota(jnp.int32, (BLOCK, 12 * gb), 1) % (4 * gb)
    picks = []
    tall = jnp.concatenate([pg[...].astype(F32)] * (BLOCK // cap), axis=0)
    tall_n = jnp.broadcast_to(pc[...].astype(F32), (BLOCK, owners))
    down = lax.broadcasted_iota(jnp.int32, (BLOCK, owners), 0)
    across = lax.broadcasted_iota(jnp.int32, (BLOCK, owners), 1)
    down_q = lax.broadcasted_iota(jnp.int32, (BLOCK, 1), 0) % rows // cap
    down_c = lax.broadcasted_iota(jnp.int32, (BLOCK, 1), 0) % cap
    for u in range(owners // GROUP):
        here = slice(u * GROUP, (u + 1) * GROUP)
        gtgt[u] = jnp.sum(jnp.where(own, full_g[here], 0.0), axis=0, keepdims=True)
        mine = across == down // rows + u * GROUP
        block = jnp.sum(jnp.where(mine, tall, 0.0), axis=1, keepdims=True).astype(jnp.int32) + down_q * gb
        count = jnp.sum(jnp.where(mine, tall_n, 0.0), axis=1, keepdims=True)
        lives = jnp.where((down_q < 3) | (down_c.astype(F32) < count), 1.0, 0.0)
        picks.append((jnp.where(wide_g == block, 1.0, 0.0).astype(BF), lives))

    for load in loads[:2]:
        load.wait()
    gtab = jnp.concatenate(
        split3(jnp.concatenate([garm[...] * SCALE, cot[...]], axis=0)), axis=0)
    for u, (hot, lives) in enumerate(picks):
        chosen = dot(hot, gtab) * lives
        for m in range(GROUP):
            send[u * GROUP + m, pl.ds(0, rows), :] = chosen[m * rows : (m + 1) * rows]
    for d in range(owners):
        send[d, pl.ds(rows, 1), :] = full_b[d : d + 1]
    pl.when(inner_i < inner - 1)(meet)

    def outgoing(k):
        return pltpu.make_async_remote_copy(
            src_ref=send.at[peer(k)], dst_ref=recv.at[me], send_sem=ssem.at[k], recv_sem=rsem.at[k],
            device_id=device(k), device_id_type=MESH)

    def returning(k):
        return pltpu.make_async_remote_copy(
            src_ref=rsend.at[peer(k)], dst_ref=rrecv.at[me], send_sem=rssem.at[k], recv_sem=rrsem.at[k],
            device_id=device(k), device_id_type=MESH)

    def table(rows_in):
        return jnp.concatenate(
            split3(jnp.concatenate([rows_in[: 3 * bb] * SCALE, rows_in[3 * bb :]], axis=0)), axis=0)

    def pushing(k):
        return pltpu.make_async_remote_copy(
            src_ref=btab, dst_ref=far.at[k - base], send_sem=xsem.at[k - base],
            recv_sem=ysem.at[k - base], device_id=device(k), device_id_type=MESH)


    row_id = lax.broadcasted_iota(jnp.int32, (rows, BLOCK), 0)
    row_c, place = row_id % cap, row_id < 3 * cap
    low_i, low_j = row_c < 2, row_c % 2 == 0
    wide = lax.broadcasted_iota(jnp.int32, (rows, 3 * 4 * bb), 1) % (4 * bb)
    slots = [jnp.concatenate([jnp.where(row_c == c, 1.0, 0.0).astype(BF)] * 6, axis=0) for c in range(cap)]

    def lhs(x, low):
        both = jnp.concatenate([jnp.where(low, x, 0.0), jnp.where(low, 0.0, x)], axis=1)
        return jnp.concatenate(split3(both), axis=0)

    def terms(x, scale):
        square = x[: 3 * cap] * x[: 3 * cap]
        norm = square[:cap] + square[cap : 2 * cap] + square[2 * cap :]
        full = jnp.concatenate([x[: 3 * cap] * scale, -norm], axis=0)
        hi = full.astype(BF).astype(F32)
        mid = (full - hi).astype(BF).astype(F32)
        low = full - hi - mid
        return [t.astype(BF) for t in (hi, mid, low, jnp.where(place, hi, 1.0), jnp.where(place, mid, 1.0))]

    def evaluate(got, row, tab):
        turned = jnp.transpose(jnp.concatenate([row, jnp.zeros((7, BLOCK), F32)], axis=0))
        onehot = jnp.where(wide == turned[:rows, 0:1].astype(jnp.int32), 1.0, 0.0).astype(BF)
        part = dot(onehot, tab)
        a1, a2, a3, a1o, a2o = terms(got, 1.0)
        b1, b2, b3, b1o, b2o = terms(part, 2.0)
        left = jnp.concatenate([a1, a2, a3, a2o, a1o, a1o], axis=0)
        right = jnp.concatenate([b1o, b2o, b1o, b1, b2, b3], axis=0)
        square = jnp.concatenate(
            [jnp.exp2(lax.dot_general(
                left, jnp.concatenate([right * slots[c], right * slots[c + 1]], axis=1),
                (((0,), (0,)), ((), ())), preferred_element_type=F32)) for c in (0, 2)], axis=0)
        k_hi = square.astype(BF)
        return part, k_hi, (square - k_hi.astype(F32)).astype(BF)

    def pull(got, part, k_hi, k_lo):
        cots = got[3 * cap :]
        stf = part[3 * cap :]
        lv = lhs(jnp.concatenate([jnp.concatenate([stf] * 3, axis=0) * part[: 3 * cap], stf], axis=0), low_j)
        rg = dot_t(lv, k_hi) + dot_t(lv, k_lo)
        rg = rg[:rows] + rg[rows : 2 * rows] + rg[2 * rows :]
        rg = jnp.where(low_i, rg[:, :BLOCK], rg[:, BLOCK:])
        sums = jnp.concatenate([rg[3 * cap :]] * 3, axis=0)
        cots3 = jnp.concatenate([cots] * 3, axis=0)
        return GRAD * (cots3 * (got[: 3 * cap] * sums - rg[: 3 * cap]))

    def process(k, got, row):
        part, k_hi, k_lo = evaluate(got, row, tab3[...])
        cots = got[3 * cap :]
        k_his[k], k_los[k] = k_hi, k_lo
        weights[k] = jnp.concatenate([jnp.concatenate([cots] * 3, axis=0) * got[: 3 * cap], cots], axis=0)
        bodies[k] = part
        return pull(got, part, k_hi, k_lo)

    def finish(k):
        part = bodies[k]
        lw = lhs(weights[k], low_i)
        rb = dot(lw, k_his[k]) + dot(lw, k_los[k])
        rb = rb[:rows] + rb[rows : 2 * rows] + rb[2 * rows :]
        rb = jnp.where(low_j, rb[:, :BLOCK], rb[:, BLOCK:])
        cols = rb[3 * cap :]
        cols3 = jnp.concatenate([cols] * 3, axis=0)
        stf3 = jnp.concatenate([part[3 * cap :]] * 3, axis=0)
        body_grad = GRAD * (stf3 * (part[: 3 * cap] * cols3 - rb[: 3 * cap]))
        parts[k] = jnp.concatenate([body_grad, amplitude * cols], axis=0)

    for bit in reversed(groups):
        pl.when(below(bit))(lambda bit=bit: each(bit, lambda j: outgoing(bit + j).start()))
    for load in loads[2:4]:
        load.wait()
    tab3[...] = table(btab[...])

    def push_last():
        for k in last:
            pushing(k).start()

    def push_prior():
        pushing(me).start()

    pl.when(outer_i == outer - 2)(push_prior)

    def raise_to(first, count, bit):
        def one(j):
            pl.semaphore_wait(ready.at[first + j], 1)
            outgoing(first + j).start()

        pl.when(jnp.logical_not(below(bit)))(lambda: each(count, one))

    recv[me, pl.ds(rows, 1), :] = send[me, pl.ds(rows, 1), :]
    rrecv[me] = process(me, send[me, pl.ds(0, rows), :], send[me, pl.ds(rows, 1), :])

    pl.when(last_row)(push_last)


    def returns(k):
        if not isinstance(k, int):
            here = jnp.logical_or(k < base, jnp.logical_and(k < base + inner, me != k))
            return jnp.logical_or(here, jnp.logical_and(k >= base + inner, jnp.logical_not(last_row)))
        return True if k < base else (me != k if k in prior else jnp.logical_not(last_row))

    def when(cond, body):
        if cond is True:
            body()
        else:
            pl.when(cond)(body)

    def arrive(ks):
        for k in ks:
            outgoing(k).wait_recv()
        grads = [process(peer(k), recv[peer(k), pl.ds(0, rows), :], recv[peer(k), pl.ds(rows, 1), :])
                 for k in ks]
        for k, grad in zip(ks, grads):
            rsend[peer(k)] = grad
        for k in ks:
            when(returns(k), lambda k=k: returning(k).start())

    for bit in groups[:-1]:
        raise_to(bit, bit, bit)
    half = owners // 2
    odd = below(half // 2)
    pl.when(odd)(lambda: raise_to(half + half // 2, half // 2, half))
    raise_to(half, half // 2, half)
    arrive([1])
    pl.when(jnp.logical_not(odd))(lambda: raise_to(half + half // 2, half // 2, half))
    each(owners // 2 - 1, lambda j: arrive([2 * j + 2, 2 * j + 3]))

    def fetch(ks):
        for k in ks:
            pushing(k).wait_recv()
        done = []
        for k in ks:
            got, row = send[peer(k), pl.ds(0, rows), :], send[peer(k), pl.ds(rows, 1), :]
            done.append(pull(got, *evaluate(got, row, table(far[k - base]))))
        for k, grad in zip(ks, done):
            rrecv[peer(k)] = grad

    each(owners, finish)

    def scatter(height, target_row, values):
        hot = jnp.where(
            lax.broadcasted_iota(jnp.int32, (height, BLOCK), 0) == target_row, 1.0, 0.0).astype(BF)
        hi, mid, lo = split3(values)
        return dot(jnp.concatenate([hot, hot, hot], axis=1), jnp.concatenate([hi, mid, lo], axis=0))

    def over_groups(one):
        total = one(0)
        for u in range(1, owners // GROUP):
            total = total + one(u)
        return total

    def body_group(u):
        target = jnp.zeros((1, BLOCK), F32)
        for m in range(GROUP):
            target = jnp.where(lane // rows == m, recv[u * GROUP + m, pl.ds(rows, 1), :], target)
        return scatter(4 * bb, target.astype(jnp.int32),
                       jnp.concatenate([parts[u * GROUP + m] for m in range(GROUP)], axis=0))

    body_sum = over_groups(body_group)
    stl[...] = body_sum[3 * bb :]
    stiff_copy = pltpu.make_async_remote_copy(
        src_ref=stl, dst_ref=strv, send_sem=fsem.at[0], recv_sem=fsem.at[1],
        device_id={"frame": 1 - frame_i}, device_id_type=MESH)
    stiff_copy.start()
    out_b[...] = body_sum[: 3 * bb]
    pl.when(head)(lambda: fetch([*prior, *last]))
    pl.when(jnp.logical_and(first_row, jnp.logical_not(head)))(lambda: fetch(last))
    each(owners - 1, lambda j: outgoing(j + 1).wait_send())
    stiff_copy.wait()
    out_s[...] = stl[...] + strv[...]
    each(base - 1, lambda j: returning(j + 1).wait_recv())

    def await_returns(ks):
        for k in ks:
            returning(k).wait_recv()

    pl.when(jnp.logical_not(head))(lambda: await_returns(prior))
    pl.when(jnp.logical_not(first_row))(lambda: await_returns(last))

    def garm_group(u):
        blank = jnp.zeros((cap, BLOCK), F32)
        pieces = []
        for m in range(GROUP):
            pieces += [rrecv[u * GROUP + m], blank]
        return scatter(3 * gb, gtgt[u].astype(jnp.int32), jnp.concatenate(pieces, axis=0))

    out_g[...] = over_groups(garm_group)
    each(owners - 1, lambda j: when(returns(j + 1), lambda: returning(j + 1).wait_send()))

    def settle_last():
        for k in last:
            pushing(k).wait_send()

    def settle_prior():
        pushing(me).wait_send()

    pl.when(last_row)(settle_last)
    pl.when(outer_i == outer - 2)(settle_prior)


def write_out(*refs):
    copies = [pltpu.make_async_copy(refs[i], refs[3 + i], refs[6].at[i]) for i in range(3)]
    for copy in copies:
        copy.start()
    for copy in copies:
        copy.wait()


def per_device(owners, inner, garment, cotangent, body_points, stiffness, pair_garment, pair_body, pair_count):
    cap = pair_garment.shape[3]
    gb, bb = garment.shape[2] // BLOCK, body_points.shape[2] // BLOCK
    rows = 4 * cap
    vmem = pl.BlockSpec(memory_space=pltpu.VMEM)
    out_g, out_b, out_s = pl.pallas_call(
        functools.partial(kernel, owners, inner, cap, gb, bb),
        out_shape=(
            jax.ShapeDtypeStruct((3 * gb, BLOCK), F32),
            jax.ShapeDtypeStruct((3 * bb, BLOCK), F32),
            jax.ShapeDtypeStruct((bb, BLOCK), F32),
        ),
        in_specs=[pl.BlockSpec(memory_space=pltpu.HBM)] * 7,
        out_specs=[vmem] * 3,
        scratch_shapes=[
            pltpu.VMEM((3 * gb, BLOCK), F32),
            pltpu.VMEM((gb, BLOCK), F32),
            pltpu.VMEM((4 * bb, BLOCK), F32),
            pltpu.VMEM((cap, owners), jnp.int32),
            pltpu.VMEM((cap, owners), jnp.int32),
            pltpu.VMEM((1, owners), jnp.int32),
            pltpu.SemaphoreType.DMA((7,)),
            pltpu.VMEM((owners, 2 * BLOCK, 2 * BLOCK), BF),
            pltpu.VMEM((owners, 2 * BLOCK, 2 * BLOCK), BF),
            pltpu.VMEM((owners, rows, BLOCK), F32),
            pltpu.VMEM((owners, rows, BLOCK), F32),
            pltpu.VMEM((owners, rows + 1, BLOCK), F32),
            pltpu.VMEM((owners, rows + 1, BLOCK), F32),
            pltpu.VMEM((owners, 3 * cap, BLOCK), F32),
            pltpu.VMEM((owners, 3 * cap, BLOCK), F32),
            pltpu.VMEM((3 * 4 * bb, BLOCK), BF),
            pltpu.VMEM((owners // GROUP, 1, BLOCK), F32),
            pltpu.VMEM((owners, rows, BLOCK), F32),
            pltpu.VMEM((bb, BLOCK), F32),
            pltpu.VMEM((bb, BLOCK), F32),
            pltpu.VMEM((2 * inner, 4 * bb, BLOCK), F32),
            pltpu.SemaphoreType.DMA((owners,)),
            pltpu.SemaphoreType.DMA((owners,)),
            pltpu.SemaphoreType.DMA((owners,)),
            pltpu.SemaphoreType.DMA((owners,)),
            pltpu.SemaphoreType.DMA((2,)),
            pltpu.SemaphoreType.DMA((2 * inner,)),
            pltpu.SemaphoreType.DMA((2 * inner,)),
            pltpu.SemaphoreType.REGULAR((owners,)),
        ],
        compiler_params=pltpu.CompilerParams(collective_id=0, has_side_effects=True,
            vmem_limit_bytes=(8 * 2**20 + owners * 5 * 2**16)),
        name="contact",
    )(
        pltpu.with_memory_space_constraint(garment.reshape(3 * gb, BLOCK), pltpu.HBM),
        pltpu.with_memory_space_constraint(cotangent.reshape(gb, BLOCK), pltpu.HBM),
        pltpu.with_memory_space_constraint(body_points.reshape(3 * bb, BLOCK), pltpu.HBM),
        pltpu.with_memory_space_constraint(stiffness.reshape(bb, BLOCK), pltpu.HBM),
        pltpu.with_memory_space_constraint(pair_garment.reshape(owners, cap).T, pltpu.HBM),
        pltpu.with_memory_space_constraint(pair_body.reshape(owners, cap).T, pltpu.HBM),
        pltpu.with_memory_space_constraint(pair_count.reshape(1, owners), pltpu.HBM),
    )
    out_g, out_b, out_s = pl.pallas_call(
        write_out,
        out_shape=tuple(jax.ShapeDtypeStruct(o.shape, o.dtype) for o in (out_g, out_b, out_s)),
        in_specs=[vmem] * 3,
        out_specs=[pl.BlockSpec(memory_space=pltpu.HBM)] * 3,
        scratch_shapes=[pltpu.SemaphoreType.DMA((3,))],
        compiler_params=pltpu.CompilerParams(vmem_limit_bytes=2**20),
        name="write_out",
    )(out_g, out_b, out_s)
    return (
        out_g.reshape(1, 3, gb * BLOCK),
        out_b.reshape(1, 3, bb * BLOCK),
        out_s.reshape(bb * BLOCK),
    )


def solution(mesh):
    inner = mesh.shape["body"]
    owners = mesh.shape["garm"] * inner
    in_specs = (
        P(("grp", "frame"), None, ("garm", "body")),
        P(("grp", "frame"), ("garm", "body")),
        P(("grp", "frame"), None, ("garm", "body")),
        P(("grp", "garm", "body")),
        P(("grp", "frame"), ("garm", "body"), None, None),
        P(("grp", "frame"), ("garm", "body"), None, None),
        P(("grp", "frame"), ("garm", "body"), None),
    )
    out_specs = (
        P(("grp", "frame"), None, ("garm", "body")),
        P(("grp", "frame"), None, ("garm", "body")),
        P(("grp", "garm", "body")),
    )
    return jax.shard_map(
        functools.partial(per_device, owners, inner),
        mesh=mesh, in_specs=in_specs, out_specs=out_specs, check_vma=False)
```
